32 devices in a mesh: narrow: 4 (over y, core), wide: 8 (over z, x).
Axes of the slice: x: 2, y: 2, z: 4, core: 2. Of those that a mesh axis runs over, the one named last changes fastest.
Arguments:
- normed: bfloat16 [1024, 2048], P('wide', 'narrow'), may hold values from -6 to 6
- router_weight: bfloat16 [2048, 128], P('narrow'), may hold values from -0.125 to 0.125
- gate_up_weight: bfloat16 [128, 2, 2048, 768], P('wide', None, 'narrow'), may hold values from -0.1875 to 0.1875
- down_weight: bfloat16 [128, 768, 2048], P('wide', 'narrow'), may hold values from -0.3125 to 0.3125
- expert_ids: int32 [1024, 8], P('wide'), may hold values from 0 to 127, all different within a row; in each aligned block of 128 rows (0 to 127, 128 to 255, ...) at most 16 rows name the same one
Outputs:
- mixed: bfloat16 [1024, 2048], P('wide', 'narrow')
The draws below stay inside these ranges and needn't reach their ends.
Inputs may be any that keep to these rules, and one draw needn't show every extreme that they name: `expert_ids`: each row names 8 different experts. In each aligned block of 128 rows (the rows of one index of wide) no expert is named by more than 16 rows, and in every draw some expert is named by exactly 16 rows of some block.
All inputs are finite; a program needn't handle non-finite values.
Results may differ from the reference program's by a relative error of at most 0.023.
Values may be sent and summed in bfloat16 or wider, within the bound.
No kernel may reach another device: no remote copies, remote signals or barrier semaphores. Data moves between devices by JAX's collectives and lax.ppermute only.
A program may use at most 128 MiB of HBM per device.

```python
import math
import jax
import jax.numpy as jnp
import numpy as np
from jax import lax

D = 2048
FF = 768
E = 128
TOPK = 8
TOK_DEV = 128
CAP = 16
TOKENS = 1024
N_NARROW = 4


def spiked(array, key, source, target, blocks, factor):
    def block_of(dim):
        return (jnp.arange(array.shape[dim]) // (array.shape[dim] // blocks)).reshape((-1,) + (1,) * (array.ndim - 1 - dim))

    near = jax.random.permutation(key, blocks)[block_of(target)]
    other_side = (block_of(target) + blocks // 2) % blocks
    return jnp.where((block_of(source) == near) | (block_of(source) == other_side), factor * array, array)


def shard_levels(stream_key, dims, pieces, least, largest):
    factor_of, own = 1.0, jax.random.fold_in(stream_key, 6)
    for axis_at, parts in pieces:
        draws = jnp.exp(jax.random.uniform(jax.random.fold_in(own, axis_at), (parts,), jnp.float32, least / len(pieces), largest / len(pieces)))
        factor_of = factor_of * jnp.repeat(draws, dims[axis_at] // parts).reshape([-1 if axis == axis_at else 1 for axis in range(len(dims))])
    return factor_of


def deal_out(stream_key, own, number, rows, amount, top, bound, lean):
    order = jax.random.permutation(stream_key, amount)
    crowded, usual = portions_of(amount, rows * top, bound, lean, True), portions_of(amount, rows * top, bound, lean, False)
    places = jnp.arange(amount)

    def named(tallies, offset_by):
        used = int((tallies > 0).sum())
        fixed = max(1, used // 4)
        moved = fixed + (places - fixed + offset_by * (used - fixed)) % max(1, amount - fixed)
        return jnp.zeros((amount,), jnp.int32).at[order[jnp.where(places < fixed, places, moved)]].set(jnp.asarray(tallies, jnp.int32))

    tallies = jnp.where(number % 4 == 0, named(crowded, number // 4), named(usual, number - number // 4 - 1))
    mixed = jax.random.permutation(jax.random.fold_in(own, 3), amount)
    donor, sink = mixed[0:amount // 2 * 2:2], mixed[1:amount // 2 * 2:2]
    slack = jnp.minimum(tallies[donor] - 1, bound - tallies[sink]) // 2
    slack = jnp.where((donor == order[0]) | (sink == order[0]) | (tallies[sink] == 0), 0, jnp.maximum(slack, 0))
    moved = jax.random.randint(jax.random.fold_in(own, 4), (amount // 2,), 0, 1 << 20) % (slack + 1)
    tallies = tallies.at[donor].add(-moved).at[sink].add(moved)
    items = jnp.searchsorted(jnp.cumsum(tallies), jnp.arange(rows * top), side="right").astype(jnp.int32)
    grid = items.reshape(top, rows).T
    grid = grid[jax.random.permutation(jax.random.fold_in(own, 1), rows)]
    offset_by = jax.random.randint(jax.random.fold_in(own, 2), (rows, 1), 0, top)
    return jnp.take_along_axis(grid, (jnp.arange(top)[None, :] + offset_by) % top, axis=1)


def portions_of(count, total, most, lean, full):
    portions = [(1 << 20) // math.isqrt(grade ** lean) + 1 for grade in range(1, count + 1)]
    largest = most if full else min(most, max(-(-total // count), total * portions[0] // sum(portions)))
    least = 1 if total - largest >= count - 1 else 0
    holding, rest = [largest] + [least] * (count - 1), total - largest - least * (count - 1)
    while rest > 0:
        movable = [i for i in range(1, count) if holding[i] < largest] or [i for i in range(1, count) if holding[i] < most]
        mass, budget = sum([portions[i] for i in movable]), rest
        for i in movable:
            addition = min(most - holding[i], max(1, budget * portions[i] // mass), rest)
            holding[i] = holding[i] + addition
            rest = rest - addition
    return np.array(holding)


def gaussian(stream_key, shape, width, bound, shards=(), kind=jnp.bfloat16):
    entries = width * jax.random.normal(stream_key, shape, jnp.float32)
    if shards:
        entries = entries * shard_levels(stream_key, shape, shards, -0.22, 0.18)
    return jnp.clip(entries, -bound, bound).astype(kind)


def gaussian_with(own_key, shape, width, most, split, heavy, kind=jnp.bfloat16):
    array = width * jax.random.normal(own_key, shape, jnp.float32)
    if split:
        array = array * shard_levels(own_key, shape, split, -0.22, 0.18)
    return jnp.clip(spiked(array, jax.random.fold_in(own_key, 3), *heavy), -most, most).astype(kind)


def setup_inputs(seed: int = 0) -> dict:
    streams_of = jax.random.split(jax.random.key(seed), 6)
    normed = gaussian(streams_of[0], (TOKENS, D), 1.0, 6.0, ((0, 8), (1, 4)))
    router_weight = gaussian(streams_of[1], (D, E), D ** -0.5, 0.125, ((0, 4),))
    gate_up_weight = gaussian_with(streams_of[2], (E, 2, D, FF), D ** -0.5, 0.1875, ((0, 8), (2, 4)), (2, 3, 4, 2.0))
    down_weight = gaussian_with(streams_of[3], (E, FF, D), FF ** -0.5, 0.3125, ((0, 8), (1, 4)), (1, 2, 4, 2.0))
    expert_ids_keys = jax.random.split(jax.random.fold_in(streams_of[4], 1), TOKENS // TOK_DEV)
    expert_ids_turns = jax.random.permutation(jax.random.fold_in(streams_of[4], 3), TOKENS // TOK_DEV)
    expert_ids = jax.vmap(lambda own, number: deal_out(jax.random.fold_in(streams_of[4], 2), own, number, TOK_DEV, E, TOPK, CAP, 2))(expert_ids_keys, expert_ids_turns).reshape((TOKENS, TOPK))
    return {"normed": normed, "router_weight": router_weight, "gate_up_weight": gate_up_weight, "down_weight": down_weight, "expert_ids": expert_ids}


def reference(normed, router_weight, gate_up_weight, down_weight, expert_ids):
    tok_total = normed.shape[0]
    blocks = tok_total // TOK_DEV
    per_block = TOK_DEV * TOPK
    logits = jnp.dot(normed, router_weight, preferred_element_type=jnp.float32)
    picker = (expert_ids[:, :, None] == jnp.arange(E, dtype=jnp.int32)[None, None, :]).astype(jnp.float32)
    chosen = jnp.sum(picker * logits[:, None, :], axis=2)
    scores = jnp.exp(chosen)
    weights = scores / jnp.sum(scores, axis=1, keepdims=True)
    pair_ids = expert_ids.reshape(blocks, per_block)
    onehot = (pair_ids[:, :, None] == jnp.arange(E, dtype=jnp.int32)[None, None, :]).astype(jnp.int32)
    running = jnp.cumsum(onehot, axis=1) - onehot
    order_in = jnp.sum(running * onehot, axis=2).astype(jnp.int32)
    block_index = jnp.arange(blocks, dtype=jnp.int32)[:, None]
    token_index = block_index * TOK_DEV + jnp.arange(per_block, dtype=jnp.int32)[None, :] // TOPK
    slot_index = ((pair_ids * blocks + block_index) * CAP + order_in).astype(jnp.int32)
    slot_count = blocks * CAP
    slot_table = jnp.full((E * slot_count,), tok_total, jnp.int32).at[slot_index.reshape(-1)].set(token_index.reshape(-1))
    padded = jnp.concatenate([normed, jnp.zeros((1, D), normed.dtype)], axis=0)

    def expert(operands):
        table_rows, gate_up, down_part = operands
        slot_rows = padded[table_rows].astype(jnp.float32).reshape(slot_count, N_NARROW, D // N_NARROW)
        partials = jnp.einsum("rqd,gqdf->gqrf", slot_rows, gate_up.astype(jnp.float32).reshape(2, N_NARROW, D // N_NARROW, FF))
        partials = lax.optimization_barrier(partials.astype(jnp.bfloat16)).astype(jnp.float32)
        summed = jnp.sum(partials, axis=1)
        hidden = (jax.nn.silu(summed[0]) * summed[1]).astype(jnp.bfloat16)
        hidden_parts = hidden.astype(jnp.float32).reshape(slot_count, N_NARROW, FF // N_NARROW)
        down_terms = jnp.einsum("rqf,qfd->qrd", hidden_parts, down_part.astype(jnp.float32).reshape(N_NARROW, FF // N_NARROW, D))
        down_terms = lax.optimization_barrier(down_terms.astype(jnp.bfloat16)).astype(jnp.float32)
        return jnp.sum(down_terms, axis=0).astype(jnp.bfloat16)

    expert_out = lax.map(expert, (slot_table.reshape(E, slot_count), gate_up_weight, down_weight))
    flat_out = expert_out.reshape(E * slot_count, D)
    slot_of_pair = slot_index.reshape(tok_total, TOPK)
    combined = jnp.zeros((tok_total, D), jnp.float32)
    for position in range(TOPK):
        combined = combined + weights[:, position, None] * flat_out[slot_of_pair[:, position]].astype(jnp.float32)
    return combined.astype(jnp.bfloat16)
```

```python
import functools

import jax
import jax.numpy as jnp
from jax import lax
from jax.experimental import pallas as pl
from jax.experimental.pallas import tpu as pltpu
from jax.sharding import PartitionSpec as P

TOPK = 8
CAP = 16
TILE = 64
ALIGN = 16
F32 = jnp.float32
BF16 = jnp.bfloat16


def swap(x, axis, mask):
    size = lax.axis_size(axis)
    return lax.ppermute(x, axis, [(i, i ^ mask) for i in range(size)])


def gate_up_kernel(place, *refs, blocks, local_experts):
    ids = refs[:blocks]
    tokens = refs[blocks:2 * blocks]
    weight = refs[2 * blocks]
    near, far, send, pos, meta, rows = refs[2 * blocks + 1:]
    e = pl.program_id(0)
    tok = ids[0].shape[1]
    total = blocks * tok

    @pl.when(e == 0)
    def _():
        lane = lax.broadcasted_iota(jnp.int32, (tok, tok), 0)
        before = (lane < lax.broadcasted_iota(jnp.int32, (tok, tok), 1)).astype(BF16)
        expert = lax.broadcasted_iota(jnp.int32, (max(local_experts, 8), tok), 0) + place[1]
        offset = jnp.zeros((max(local_experts, 8), 1), F32)
        ranks, hots = [], []
        for b in range(blocks):
            rows[b * tok:(b + 1) * tok, :] = tokens[b][...]
            hot = jnp.zeros(expert.shape, F32)
            for k in range(TOPK):
                hot = jnp.where(ids[b][k:k + 1, :] == expert, 1.0, hot)
            ranks.append(jnp.dot(hot.astype(BF16), before, preferred_element_type=F32) + offset)
            hots.append(hot)
            offset = offset + jnp.sum(hot, axis=1, keepdims=True)
        base = jnp.int32(0)
        for i in range(local_experts):
            count = jnp.sum(offset[i:i + 1, :]).astype(jnp.int32)
            meta[0, i] = base
            meta[1, i] = count
            for b in range(blocks):
                pos[i:i + 1, b * tok:(b + 1) * tok] = jnp.where(
                    hots[b][i:i + 1] > 0.0, ranks[b][i:i + 1].astype(jnp.int32) + base, -1)
            base = base + (count + ALIGN - 1) // ALIGN * ALIGN
        meta[2, 0] = base

    first = meta[0, e]
    at = pos[pl.ds(e, 1), :]
    mine = place[0]
    flip_core = (mine & 1) == 1
    flip_chip = (mine & 2) == 2

    def tile(j, carry):
        start = pl.multiple_of(first + j * TILE, ALIGN)
        pick = (lax.broadcasted_iota(jnp.int32, (TILE, total), 0) + start == at)
        x = jnp.dot(pick.astype(F32).astype(BF16), rows[...], preferred_element_type=F32).astype(BF16)
        g = jnp.dot(x, weight[0, 0], preferred_element_type=F32)
        u = jnp.dot(x, weight[0, 1], preferred_element_type=F32)
        quarter = g.shape[1] // 4
        d = [jnp.concatenate([g[:, q * quarter:(q + 1) * quarter], u[:, q * quarter:(q + 1) * quarter]], axis=1)
             for q in range(4)]
        d = [jnp.where(flip_core, d[q ^ 1], d[q]) for q in range(4)]
        d = [jnp.where(flip_chip, d[q ^ 2], d[q]).astype(BF16) for q in range(4)]
        near[pl.ds(start, TILE), :] = d[0]
        send[0, pl.ds(start, TILE), :] = d[1]
        far[pl.ds(start, TILE), :] = d[2]
        send[1, pl.ds(start, TILE), :] = d[3]
        return carry

    lax.fori_loop(0, (meta[1, e] + TILE - 1) // TILE, tile, 0)


def gate_up(place, ids, tokens, weight, rows_cap):
    blocks = len(ids)
    tok, width = tokens[0].shape
    local_experts, _, _, units = weight.shape
    full = lambda shape: pl.BlockSpec(shape, lambda e, *_: (0,) * len(shape))
    half = units // 2
    grid_spec = pltpu.PrefetchScalarGridSpec(
        num_scalar_prefetch=1,
        grid=(local_experts,),
        in_specs=[full(i.shape) for i in ids] + [full(t.shape) for t in tokens]
        + [pl.BlockSpec((1,) + weight.shape[1:], lambda e, *_: (e, 0, 0, 0))],
        out_specs=[full((rows_cap, half)), full((rows_cap, half)), full((2, rows_cap, half)),
                   full((local_experts, blocks * tok)),
                   pl.BlockSpec(memory_space=pltpu.SMEM)],
        scratch_shapes=[pltpu.VMEM((blocks * tok, width), BF16)],
    )
    return pl.pallas_call(
        functools.partial(gate_up_kernel, blocks=blocks, local_experts=local_experts),
        grid_spec=grid_spec,
        out_shape=[jax.ShapeDtypeStruct((rows_cap, half), BF16), jax.ShapeDtypeStruct((rows_cap, half), BF16),
                   jax.ShapeDtypeStruct((2, rows_cap, half), BF16),
                   jax.ShapeDtypeStruct((local_experts, blocks * tok), jnp.int32),
                   jax.ShapeDtypeStruct((3, max(local_experts, 8)), jnp.int32)],
        compiler_params=pltpu.CompilerParams(vmem_limit_bytes=48 * 1024 * 1024),
        name="gate_up",
    )(place, *ids, *tokens, weight)


def down_kernel(place, meta, *refs, blocks, local_experts):
    ids = refs[:blocks]
    scores = refs[blocks:2 * blocks]
    pos, near, beside, across, weight, keep, far, send, terms, picks, picks_t, share = refs[2 * blocks:]
    e = pl.program_id(0)
    tok = ids[0].shape[1]
    total = blocks * tok
    cap = near.shape[0]
    width = keep.shape[1]

    @pl.when(e == 0)
    def _():
        expert = lax.broadcasted_iota(jnp.int32, (max(local_experts, 8), tok), 0) + place[1]
        for b in range(blocks):
            value = jnp.zeros(expert.shape, F32)
            for k in range(TOPK):
                value = jnp.where(ids[b][k:k + 1, :] == expert, scores[b][k:k + 1, :], value)
            share[:, b * tok:(b + 1) * tok] = value

        def clear(j, carry):
            start = pl.multiple_of(j * TILE, TILE)
            for q in range(4):
                terms[q, pl.ds(start, TILE), :] = jnp.zeros((TILE, width), BF16)
            picks[pl.ds(start, TILE), :] = jnp.zeros((TILE, total), BF16)
            return carry

        lax.fori_loop(meta[2, 0] // TILE, cap // TILE, clear, 0)

    first = meta[0, e]
    at = pos[pl.ds(e, 1), :]
    part = share[pl.ds(e, 1), :]

    def tile(j, carry):
        start = pl.multiple_of(first + j * TILE, ALIGN)
        pick = (lax.broadcasted_iota(jnp.int32, (TILE, total), 0) + start == at)
        picks[pl.ds(start, TILE), :] = pick.astype(F32).astype(BF16)
        scale = jnp.sum(jnp.where(pick, part, 0.0), axis=1, keepdims=True)
        s = (near[pl.ds(start, TILE), :].astype(F32) + beside[0, pl.ds(start, TILE), :].astype(F32)
             + across[pl.ds(start, TILE), :].astype(F32))
        half = s.shape[1] // 2
        g = s[:, :half]
        h = (g / (1.0 + jnp.exp(-g)) * s[:, half:] * scale).astype(BF16)
        t = jnp.dot(h, weight[0], preferred_element_type=F32).astype(BF16)
        for q in range(4):
            terms[q, pl.ds(start, TILE), :] = t[:, q * width:(q + 1) * width]
        return carry

    lax.fori_loop(0, (meta[1, e] + TILE - 1) // TILE, tile, 0)

    @pl.when(e == local_experts - 1)
    def _():
        mine = place[0]
        picks_t[...] = picks[...].T
        send[0] = jnp.dot(picks_t[...], terms[mine ^ 1], preferred_element_type=F32).astype(BF16)
        send[1] = jnp.dot(picks_t[...], terms[mine ^ 3], preferred_element_type=F32).astype(BF16)
        far[...] = jnp.dot(picks_t[...], terms[mine ^ 2], preferred_element_type=F32).astype(BF16)
        keep[...] = jnp.dot(picks_t[...], terms[mine], preferred_element_type=F32).astype(BF16)


def down(place, meta, ids, scores, pos, near, beside, across, weight, width):
    blocks = len(ids)
    tok = ids[0].shape[1]
    local_experts = weight.shape[0]
    cap = near.shape[0]
    total = blocks * tok
    full = lambda shape: pl.BlockSpec(shape, lambda e, *_: (0,) * len(shape))
    grid_spec = pltpu.PrefetchScalarGridSpec(
        num_scalar_prefetch=2,
        grid=(local_experts,),
        in_specs=[full(i.shape) for i in ids] + [full(s.shape) for s in scores]
        + [full(pos.shape), full(near.shape), full((1,) + beside.shape[1:]), full(across.shape),
           pl.BlockSpec((1,) + weight.shape[1:], lambda e, *_: (e, 0, 0))],
        out_specs=[full((total, width)), full((total, width)), full((2, total, width))],
        scratch_shapes=[pltpu.VMEM((4, cap, width), BF16), pltpu.VMEM((cap, total), BF16),
                        pltpu.VMEM((total, cap), BF16), pltpu.VMEM((max(local_experts, 8), total), F32)],
    )
    return pl.pallas_call(
        functools.partial(down_kernel, blocks=blocks, local_experts=local_experts),
        grid_spec=grid_spec,
        out_shape=[jax.ShapeDtypeStruct((total, width), BF16), jax.ShapeDtypeStruct((total, width), BF16),
                   jax.ShapeDtypeStruct((2, total, width), BF16)],
        compiler_params=pltpu.CompilerParams(vmem_limit_bytes=56 * 1024 * 1024),
        name="down",
    )(place, meta, *ids, *scores, pos, near, beside, across, weight)


def add(*parts):
    total = parts[0].astype(F32)
    for part in parts[1:]:
        total = total + part.astype(F32)
    return total.astype(BF16)


def gather_wide(x, size):
    pieces = {0: x}
    bit = size // 2
    while bit:
        pieces.update({j | bit: swap(p, "wide", bit) for j, p in list(pieces.items())})
        bit //= 2
    return [pieces[j] for j in range(size)]


def local(normed, router_weight, gate_up_weight, down_weight, expert_ids):
    tok, width = normed.shape
    experts = router_weight.shape[1]
    local_experts = gate_up_weight.shape[0]
    size = lax.axis_size("wide")
    mine = lax.axis_index("narrow")
    place = jnp.stack([mine, lax.axis_index("wide") * local_experts]).astype(jnp.int32)
    ids_t = expert_ids.T
    ids = gather_wide(ids_t, size)
    tokens = gather_wide(normed, size)

    partial = lax.dot_general(router_weight, normed, (((0,), (1,)), ((), ())),
                              preferred_element_type=F32).astype(BF16)
    logits = partial.astype(F32)
    for mask in (1, 2, 3):
        logits = logits + swap(partial, "narrow", mask).astype(F32)
    hot = ids_t[:, None, :] == jnp.arange(experts, dtype=jnp.int32)[None, :, None]
    chosen = jnp.sum(jnp.where(hot, logits[None], 0.0), axis=1)
    scores = jnp.exp(chosen)
    scores = gather_wide(scores / jnp.sum(scores, axis=0, keepdims=True), size)

    group = min(size, 8)
    groups = size // group
    rows_cap = local_experts * group * CAP
    results = []
    for c in range(groups):
        own = slice(c * group, (c + 1) * group)
        near, far, send, pos, meta = gate_up(place, ids[own], tokens[own], gate_up_weight, rows_cap)
        beside = swap(send, "narrow", 1)
        across = swap(add(far, beside[1]), "narrow", 2)
        keep, far, send = down(place, meta, ids[own], scores[own], pos, near, beside, across, down_weight, width)
        beside = swap(send, "narrow", 1)
        across = swap(add(far, beside[1]), "narrow", 2)
        results.append((keep, beside[0], across))
    pieces = [add(*(r[(j % group) * tok:(j % group + 1) * tok] for r in results[j // group])) for j in range(size)]
    bit = 1
    while bit < size:
        moved = {j: swap(pieces[j], "wide", bit) for j in range(size) if j % (2 * bit) == bit}
        pieces = [add(p, moved[j | bit]) if j % (2 * bit) == 0 else None for j, p in enumerate(pieces)]
        bit *= 2
    return pieces[0]


def solution(mesh):
    placed = (
        P("wide", "narrow"),
        P("narrow", None),
        P("wide", None, "narrow", None),
        P("wide", "narrow", None),
        P("wide", None),
    )
    return jax.shard_map(
        local, mesh=mesh, in_specs=placed, out_specs=P("wide", "narrow"), check_vma=False
    )
```

```python
import functools

import jax
import jax.numpy as jnp
from jax import lax
from jax.experimental import pallas as pl
from jax.experimental.pallas import tpu as pltpu
from jax.sharding import PartitionSpec as P


TOPK = 8
CAP = 16
GROUP = 4
TILE = GROUP * CAP
ALIGN = 16
F32 = jnp.float32
BF16 = jnp.bfloat16


def swap(x, axis, mask):
    size = lax.axis_size(axis)
    return lax.ppermute(x, axis, [(i, i ^ mask) for i in range(size)])


def gate_up_kernel(place, ids, tokens, router, weight, near, far, send, pos, meta, buffer, arrived, *,
                   blocks, local_experts):
    total = tokens.shape[0]
    tok = total // blocks
    copies = [pltpu.make_async_copy(weight.at[e], buffer.at[e], arrived.at[e]) for e in range(local_experts)]
    for copy in copies:
        copy.start()

    lane = lax.broadcasted_iota(jnp.int32, (tok, tok), 0)
    before = (lane < lax.broadcasted_iota(jnp.int32, (tok, tok), 1)).astype(BF16)
    expert = lax.broadcasted_iota(jnp.int32, (max(local_experts, 8), tok), 0) + place[1]
    every = lax.broadcasted_iota(jnp.int32, (router.shape[1], tok), 0)
    offset = jnp.zeros((max(local_experts, 8), 1), F32)
    ranks, hots, chosen = [], [], []
    for b in range(blocks):
        hot = jnp.zeros(expert.shape, F32)
        logits = jnp.dot(tokens[b * tok:(b + 1) * tok, :], router[...], preferred_element_type=F32).T
        for k in range(TOPK):
            row = ids[b * TOPK + k:b * TOPK + k + 1, :]
            hot = jnp.where(row == expert, 1.0, hot)
            chosen.append(jnp.sum(jnp.where(row == every, logits, 0.0), axis=0, keepdims=True))
        ranks.append(jnp.dot(hot.astype(BF16), before, preferred_element_type=F32) + offset)
        hots.append(hot)
        offset = offset + jnp.sum(hot, axis=1, keepdims=True)
    slots = local_experts * TILE
    extra = jnp.concatenate(
        [jnp.concatenate(chosen[2 * TOPK * p:2 * TOPK * (p + 1)], axis=0) for p in range(blocks // 2)]
        + [jnp.zeros((2 * TOPK, near.shape[1] - tok * (blocks // 2)), F32)], axis=1).astype(BF16)
    near[slots:, :] = extra
    far[slots:, :] = extra
    send[0, slots:, :] = extra
    send[1, slots:, :] = extra

    rank = jnp.concatenate(ranks, axis=1).astype(jnp.int32)
    hot = jnp.concatenate(hots, axis=1)
    mine = place[0]
    flip_core = (mine & 1) == 1
    flip_chip = (mine & 2) == 2
    slot = lax.broadcasted_iota(jnp.int32, (TILE, total), 0)
    start = jnp.int32(0)
    for e in range(local_experts):
        count = jnp.sum(offset[e:e + 1, :]).astype(jnp.int32)
        at = jnp.where(hot[e:e + 1] > 0.0, rank[e:e + 1], -1)
        pos[e:e + 1, :] = at
        meta[e] = start
        start = pl.multiple_of(start, ALIGN)
        pick = (slot == at).astype(F32).astype(BF16)
        x = jnp.dot(pick, tokens[...], preferred_element_type=F32).astype(BF16)
        copies[e].wait()
        g = jnp.dot(x, buffer[e, 0], preferred_element_type=F32)
        u = jnp.dot(x, buffer[e, 1], preferred_element_type=F32)
        quarter = g.shape[1] // 4
        d = [jnp.concatenate([g[:, q * quarter:(q + 1) * quarter], u[:, q * quarter:(q + 1) * quarter]], axis=1)
             for q in range(4)]
        d = [jnp.where(flip_core, d[q ^ 1], d[q]) for q in range(4)]
        d = [jnp.where(flip_chip, d[q ^ 2], d[q]).astype(BF16) for q in range(4)]
        near[pl.ds(start, TILE), :] = d[0]
        send[0, pl.ds(start, TILE), :] = d[1]
        far[pl.ds(start, TILE), :] = d[2]
        send[1, pl.ds(start, TILE), :] = d[3]
        start = start + (count + ALIGN - 1) // ALIGN * ALIGN


VMEM = pl.BlockSpec(memory_space=pltpu.VMEM)
SMEM = pl.BlockSpec(memory_space=pltpu.SMEM)
HBM = pl.BlockSpec(memory_space=pltpu.HBM)


def gate_up(place, ids, tokens, router, weight, blocks):
    total, width = tokens.shape
    local_experts, _, _, units = weight.shape
    half = units // 2
    rows = local_experts * TILE + 2 * TOPK
    return pl.pallas_call(
        functools.partial(gate_up_kernel, blocks=blocks, local_experts=local_experts),
        in_specs=[SMEM, VMEM, VMEM, VMEM, HBM],
        out_specs=[VMEM, VMEM, VMEM, VMEM, SMEM],
        scratch_shapes=[pltpu.VMEM(weight.shape, BF16), pltpu.SemaphoreType.DMA((local_experts,))],
        out_shape=[jax.ShapeDtypeStruct((rows, half), BF16), jax.ShapeDtypeStruct((rows, half), BF16),
                   jax.ShapeDtypeStruct((2, rows, half), BF16),
                   jax.ShapeDtypeStruct((max(local_experts, 8), total), jnp.int32),
                   jax.ShapeDtypeStruct((max(local_experts, 8),), jnp.int32)],
        compiler_params=pltpu.CompilerParams(vmem_limit_bytes=36 * 1024 * 1024),
        cost_estimate=pl.CostEstimate(flops=6 * rows * width * units, bytes_accessed=2 * weight.size,
                                      transcendentals=0),
        name="gate_up",
    )(place, ids, tokens, router, weight)


def down_kernel(place, meta, ids, pos, near, beside, across, weight, keep, far, send,
                terms, picks, picks_t, buffer, arrived, *, blocks, local_experts):
    total, width = keep.shape
    tok = total // blocks
    cap = local_experts * TILE
    copies = [pltpu.make_async_copy(weight.at[e], buffer.at[e], arrived.at[e]) for e in range(local_experts)]
    for copy in copies:
        copy.start()

    expert = lax.broadcasted_iota(jnp.int32, (max(local_experts, 8), tok), 0) + place[1]
    extra = near[cap:, :].astype(F32) + beside[0, cap:, :].astype(F32) + across[cap:, :].astype(F32)
    values = []
    for b in range(blocks):
        scores = jnp.exp(extra[b % 2 * TOPK:(b % 2 + 1) * TOPK, b // 2 * tok:(b // 2 + 1) * tok])
        scores = scores / jnp.sum(scores, axis=0, keepdims=True)
        value = jnp.zeros(expert.shape, F32)
        for k in range(TOPK):
            row = ids[b * TOPK + k:b * TOPK + k + 1, :]
            value = jnp.where(row == expert, scores[k:k + 1, :], value)
        values.append(value)
    share = jnp.concatenate(values, axis=1)

    def clear(j, carry):
        start = pl.multiple_of(j * TILE, TILE)
        for q in range(4):
            terms[q, pl.ds(start, TILE), :] = jnp.zeros((TILE, width), BF16)
        picks[pl.ds(start, TILE), :] = jnp.zeros((TILE, total), BF16)
        return carry

    lax.fori_loop(meta[local_experts - 1] // TILE, cap // TILE, clear, 0)
    slot = lax.broadcasted_iota(jnp.int32, (TILE, total), 0)
    for e in range(local_experts):
        start = pl.multiple_of(meta[e], ALIGN)
        pick = slot == pos[e:e + 1, :]
        picks[pl.ds(start, TILE), :] = pick.astype(F32).astype(BF16)
        scale = jnp.sum(jnp.where(pick, share[e:e + 1], 0.0), axis=1, keepdims=True)
        s = (near[pl.ds(start, TILE), :].astype(F32) + beside[0, pl.ds(start, TILE), :].astype(F32)
             + across[pl.ds(start, TILE), :].astype(F32))
        half = s.shape[1] // 2
        g = s[:, :half]
        h = (g / (1.0 + jnp.exp(-g)) * s[:, half:] * scale).astype(BF16)
        copies[e].wait()
        t = jnp.dot(h, buffer[e], preferred_element_type=F32).astype(BF16)
        for q in range(4):
            terms[q, pl.ds(start, TILE), :] = t[:, q * width:(q + 1) * width]

    mine = place[0]
    picks_t[...] = picks[...].T
    send[0] = jnp.dot(picks_t[...], terms[mine ^ 1], preferred_element_type=F32).astype(BF16)
    send[1] = jnp.dot(picks_t[...], terms[mine ^ 3], preferred_element_type=F32).astype(BF16)
    far[...] = jnp.dot(picks_t[...], terms[mine ^ 2], preferred_element_type=F32).astype(BF16)
    keep[...] = jnp.dot(picks_t[...], terms[mine], preferred_element_type=F32).astype(BF16)


def down(place, meta, ids, pos, near, beside, across, weight, blocks, tok, width):
    local_experts = weight.shape[0]
    cap = local_experts * TILE
    total = blocks * tok
    return pl.pallas_call(
        functools.partial(down_kernel, blocks=blocks, local_experts=local_experts),
        in_specs=[SMEM, SMEM] + [VMEM] * 5 + [HBM],
        out_specs=[VMEM, VMEM, VMEM],
        scratch_shapes=[pltpu.VMEM((4, cap, width), BF16), pltpu.VMEM((cap, total), BF16),
                        pltpu.VMEM((total, cap), BF16), pltpu.VMEM(weight.shape, BF16),
                        pltpu.SemaphoreType.DMA((local_experts,))],
        out_shape=[jax.ShapeDtypeStruct((total, width), BF16), jax.ShapeDtypeStruct((total, width), BF16),
                   jax.ShapeDtypeStruct((2, total, width), BF16)],
        compiler_params=pltpu.CompilerParams(vmem_limit_bytes=36 * 1024 * 1024),
        cost_estimate=pl.CostEstimate(flops=8 * total * cap * width, bytes_accessed=2 * weight.size,
                                      transcendentals=0),
        name="down",
    )(place, meta, ids, pos, near, beside, across, weight)


def add(*parts):
    total = parts[0].astype(F32)
    for part in parts[1:]:
        total = total + part.astype(F32)
    return total.astype(BF16)


def gather_wide(x, size):
    chunks, order = [x], [[0]]
    bit = size // 2
    while bit:
        moved = [swap(p, "wide", bit) for p in chunks]
        flipped = [[j | bit for j in o] for o in order]
        if len(order[0]) < GROUP:
            chunks, order = [jnp.concatenate([chunks[0], moved[0]], axis=0)], [order[0] + flipped[0]]
        else:
            chunks, order = chunks + moved, order + flipped
        bit //= 2
    return chunks, order


def local(normed, router_weight, gate_up_weight, down_weight, expert_ids):
    tok, width = normed.shape
    local_experts = gate_up_weight.shape[0]
    size = lax.axis_size("wide")
    mine = lax.axis_index("narrow")
    place = jnp.stack([mine, lax.axis_index("wide") * local_experts]).astype(jnp.int32)
    ids, _ = gather_wide(expert_ids.T, size)
    tokens, order = gather_wide(normed, size)

    stage = []
    for c in range(len(order)):
        near, far, send, pos, meta = gate_up(place, ids[c], tokens[c], router_weight, gate_up_weight, GROUP)
        beside = swap(send, "narrow", 1)
        far = add(far, beside[1])
        across = swap(far, "narrow", 2)
        stage.append((near, beside, across, pos, meta))
    terms = []
    for c in range(len(order)):
        near, beside, across, pos, meta = stage[c]
        keep, far, send = down(place, meta, ids[c], pos, near, beside, across, down_weight, GROUP, tok, width)
        beside = swap(send, "narrow", 1)
        far = add(far, beside[1])
        across = swap(far, "narrow", 2)
        whole = add(keep, beside[0], across)
        for i, j in enumerate(order[c]):
            piece = whole[i * tok:(i + 1) * tok]
            terms.append(swap(piece, "wide", j) if j else piece)
    return add(*terms)


def solution(mesh):
    placed = (
        P("wide", "narrow"),
        P("narrow", None),
        P("wide", None, "narrow", None),
        P("wide", "narrow", None),
        P("wide", None),
    )

    return jax.shard_map(local, mesh=mesh, in_specs=placed, out_specs=P("wide", "narrow"), check_vma=False)
```

```python
import functools

import jax
import jax.numpy as jnp
from jax import lax
from jax.experimental import pallas as pl
from jax.experimental.pallas import tpu as pltpu
from jax.sharding import PartitionSpec as P


TOPK = 8
CAP = 16
GROUP = 4
PARTS = 2
GATE_VMEM = 40
DOWN_VMEM = 54
TILE = GROUP * CAP
ALIGN = 16
F32 = jnp.float32
BF16 = jnp.bfloat16


def swap(x, axis, mask):
    size = lax.axis_size(axis)
    return lax.ppermute(x, axis, [(i, i ^ mask) for i in range(size)])


def gate_up_kernel(place, *refs, blocks, local_experts):
    block, (router, weight, near, far, send, pos, ids, meta, tokens, buffer, arrived) = refs[:blocks], refs[blocks:]
    total = tokens.shape[0]
    tok = total // blocks
    copies = [pltpu.make_async_copy(weight.at[e], buffer.at[e], arrived.at[e]) for e in range(local_experts)]
    for copy in copies:
        copy.start()

    lane = lax.broadcasted_iota(jnp.int32, (tok, tok), 0)
    before = (lane < lax.broadcasted_iota(jnp.int32, (tok, tok), 1)).astype(BF16)
    expert = lax.broadcasted_iota(jnp.int32, (max(local_experts, 8), tok), 0) + place[1]
    every = lax.broadcasted_iota(jnp.int32, (router.shape[1], tok), 0)
    offset = jnp.zeros((max(local_experts, 8), 1), F32)
    ranks, hots, chosen = [], [], []
    for b in range(blocks):
        hot = jnp.zeros(expert.shape, F32)
        tokens[b * tok:(b + 1) * tok, :] = block[b][:tok, :]
        ids[b * TOPK:(b + 1) * TOPK, :] = block[b][tok:, :tok].astype(F32).astype(jnp.int32)
        logits = jnp.dot(tokens[b * tok:(b + 1) * tok, :], router[...], preferred_element_type=F32).T
        for k in range(TOPK):
            row = ids[b * TOPK + k:b * TOPK + k + 1, :]
            hot = jnp.where(row == expert, 1.0, hot)
            chosen.append(jnp.sum(jnp.where(row == every, logits, 0.0), axis=0, keepdims=True))
        ranks.append(jnp.dot(hot.astype(BF16), before, preferred_element_type=F32) + offset)
        hots.append(hot)
        offset = offset + jnp.sum(hot, axis=1, keepdims=True)
    slots = local_experts * TILE
    extra = jnp.concatenate(
        [jnp.concatenate(chosen[2 * TOPK * p:2 * TOPK * (p + 1)], axis=0) for p in range(blocks // 2)]
        + [jnp.zeros((2 * TOPK, near.shape[1] - tok * (blocks // 2)), F32)], axis=1).astype(BF16)
    near[slots:, :] = extra
    far[slots:, :] = extra
    send[0, slots:, :] = extra
    send[1, slots:, :] = extra

    rank = jnp.concatenate(ranks, axis=1).astype(jnp.int32)
    hot = jnp.concatenate(hots, axis=1)
    mine = place[0]
    flip_core = (mine & 1) == 1
    flip_chip = (mine & 2) == 2
    slot = lax.broadcasted_iota(jnp.int32, (TILE, total), 0)
    start = jnp.int32(0)
    for e in range(local_experts):
        count = jnp.sum(offset[e:e + 1, :]).astype(jnp.int32)
        at = jnp.where(hot[e:e + 1] > 0.0, rank[e:e + 1], -1)
        pos[e:e + 1, :] = at
        meta[e] = start
        start = pl.multiple_of(start, ALIGN)
        pick = (slot == at).astype(F32).astype(BF16)
        x = jnp.dot(pick, tokens[...], preferred_element_type=F32).astype(BF16)
        copies[e].wait()
        g = jnp.dot(x, buffer[e, 0], preferred_element_type=F32)
        u = jnp.dot(x, buffer[e, 1], preferred_element_type=F32)
        quarter = g.shape[1] // 4
        d = [jnp.concatenate([g[:, q * quarter:(q + 1) * quarter], u[:, q * quarter:(q + 1) * quarter]], axis=1)
             for q in range(4)]
        d = [jnp.where(flip_core, d[q ^ 1], d[q]) for q in range(4)]
        d = [jnp.where(flip_chip, d[q ^ 2], d[q]).astype(BF16) for q in range(4)]
        near[pl.ds(start, TILE), :] = d[0]
        send[0, pl.ds(start, TILE), :] = d[1]
        far[pl.ds(start, TILE), :] = d[2]
        send[1, pl.ds(start, TILE), :] = d[3]
        start = start + (count + ALIGN - 1) // ALIGN * ALIGN


VMEM = pl.BlockSpec(memory_space=pltpu.VMEM)
SMEM = pl.BlockSpec(memory_space=pltpu.SMEM)
HBM = pl.BlockSpec(memory_space=pltpu.HBM)


def gate_up(place, block, router, weight, tok):
    blocks = len(block)
    total, width = blocks * tok, block[0].shape[1]
    local_experts, _, _, units = weight.shape
    half = units // 2
    rows = local_experts * TILE + 2 * TOPK
    return pl.pallas_call(
        functools.partial(gate_up_kernel, blocks=blocks, local_experts=local_experts),
        in_specs=[SMEM] + [VMEM] * (blocks + 1) + [HBM],
        out_specs=[VMEM, VMEM, VMEM, VMEM, VMEM, SMEM],
        scratch_shapes=[pltpu.VMEM((total, width), BF16), pltpu.VMEM(weight.shape, BF16),
                        pltpu.SemaphoreType.DMA((local_experts,))],
        out_shape=[jax.ShapeDtypeStruct((rows, half), BF16), jax.ShapeDtypeStruct((rows, half), BF16),
                   jax.ShapeDtypeStruct((2, rows, half), BF16),
                   jax.ShapeDtypeStruct((max(local_experts, 8), total), jnp.int32),
                   jax.ShapeDtypeStruct((blocks * TOPK, tok), jnp.int32),
                   jax.ShapeDtypeStruct((max(local_experts, 8),), jnp.int32)],
        compiler_params=pltpu.CompilerParams(vmem_limit_bytes=GATE_VMEM * 1024 * 1024),
        cost_estimate=pl.CostEstimate(flops=6 * rows * width * units, bytes_accessed=2 * weight.size,
                                      transcendentals=0),
        name="gate_up",
    )(place, *block, router, weight)


def down_kernel(place, meta, ids, pos, near, beside, across, weight, keep, far, send,
                terms, picks, picks_t, buffer, arrived, *, blocks, local_experts):
    total, width = keep.shape
    tok = total // blocks
    cap = local_experts * TILE
    copies = [pltpu.make_async_copy(weight.at[e], buffer.at[e], arrived.at[e]) for e in range(local_experts)]
    for copy in copies:
        copy.start()

    expert = lax.broadcasted_iota(jnp.int32, (max(local_experts, 8), tok), 0) + place[1]
    extra = near[cap:, :].astype(F32) + beside[0, cap:, :].astype(F32) + across[cap:, :].astype(F32)
    values = []
    for b in range(blocks):
        scores = jnp.exp(extra[b % 2 * TOPK:(b % 2 + 1) * TOPK, b // 2 * tok:(b // 2 + 1) * tok])
        scores = scores / jnp.sum(scores, axis=0, keepdims=True)
        value = jnp.zeros(expert.shape, F32)
        for k in range(TOPK):
            row = ids[b * TOPK + k:b * TOPK + k + 1, :]
            value = jnp.where(row == expert, scores[k:k + 1, :], value)
        values.append(value)
    share = jnp.concatenate(values, axis=1)

    def clear(j, carry):
        start = pl.multiple_of(j * TILE, TILE)
        for q in range(4):
            terms[q, pl.ds(start, TILE), :] = jnp.zeros((TILE, width), BF16)
        picks[pl.ds(start, TILE), :] = jnp.zeros((TILE, total), BF16)
        return carry

    lax.fori_loop(meta[local_experts - 1] // TILE, cap // TILE, clear, 0)
    slot = lax.broadcasted_iota(jnp.int32, (TILE, total), 0)
    for e in range(local_experts):
        start = pl.multiple_of(meta[e], ALIGN)
        pick = slot == pos[e:e + 1, :]
        picks[pl.ds(start, TILE), :] = pick.astype(F32).astype(BF16)
        scale = jnp.sum(jnp.where(pick, share[e:e + 1], 0.0), axis=1, keepdims=True)
        s = (near[pl.ds(start, TILE), :].astype(F32) + beside[0, pl.ds(start, TILE), :].astype(F32)
             + across[pl.ds(start, TILE), :].astype(F32))
        half = s.shape[1] // 2
        g = s[:, :half]
        h = (g / (1.0 + jnp.exp(-g)) * s[:, half:] * scale).astype(BF16)
        copies[e].wait()
        t = jnp.dot(h, buffer[e], preferred_element_type=F32).astype(BF16)
        for q in range(4):
            terms[q, pl.ds(start, TILE), :] = t[:, q * width:(q + 1) * width]

    mine = place[0]
    picks_t[...] = picks[...].T
    send[0] = jnp.dot(picks_t[...], terms[mine ^ 1], preferred_element_type=F32).astype(BF16)
    send[1] = jnp.dot(picks_t[...], terms[mine ^ 3], preferred_element_type=F32).astype(BF16)
    far[...] = jnp.dot(picks_t[...], terms[mine ^ 2], preferred_element_type=F32).astype(BF16)
    keep[...] = jnp.dot(picks_t[...], terms[mine], preferred_element_type=F32).astype(BF16)


def down(place, meta, ids, pos, near, beside, across, weight, blocks, tok, width):
    local_experts = weight.shape[0]
    cap = local_experts * TILE
    total = blocks * tok
    return pl.pallas_call(
        functools.partial(down_kernel, blocks=blocks, local_experts=local_experts),
        in_specs=[SMEM, SMEM] + [VMEM] * 5 + [HBM],
        out_specs=[VMEM, VMEM, VMEM],
        scratch_shapes=[pltpu.VMEM((4, cap, width), BF16), pltpu.VMEM((cap, total), BF16),
                        pltpu.VMEM((total, cap), BF16), pltpu.VMEM(weight.shape, BF16),
                        pltpu.SemaphoreType.DMA((local_experts,))],
        out_shape=[jax.ShapeDtypeStruct((total, width), BF16), jax.ShapeDtypeStruct((total, width), BF16),
                   jax.ShapeDtypeStruct((2, total, width), BF16)],
        compiler_params=pltpu.CompilerParams(vmem_limit_bytes=DOWN_VMEM * 1024 * 1024),
        cost_estimate=pl.CostEstimate(flops=8 * total * cap * width, bytes_accessed=2 * weight.size,
                                      transcendentals=0),
        name="down",
    )(place, meta, ids, pos, near, beside, across, weight)


def add(*parts):
    total = parts[0].astype(F32)
    for part in parts[1:]:
        total = total + part.astype(F32)
    return total.astype(BF16)


def gather_wide(x, size):
    pieces = {0: x}
    bit = size // 2
    while bit:
        for j, p in list(pieces.items()):
            pieces[j | bit] = swap(p, "wide", bit)
        bit //= 2
    return pieces


def local(normed, router_weight, gate_up_weight, down_weight, expert_ids):
    tok, width = normed.shape
    local_experts = gate_up_weight.shape[0]
    size = lax.axis_size("wide")
    mine = lax.axis_index("narrow")
    place = jnp.stack([mine, lax.axis_index("wide") * local_experts]).astype(jnp.int32)
    ids = jnp.pad(expert_ids.T.astype(BF16), ((0, 0), (0, width - tok)))
    pieces = gather_wide(jnp.concatenate([normed, ids], axis=0), size)
    groups = size // GROUP
    order = [[c + groups * i for i in range(GROUP)] for c in range(groups)]

    stage = []
    for c in range(groups):
        near, far, send, pos, ids, meta = gate_up(
            place, [pieces[j] for j in order[c]], router_weight, gate_up_weight, tok)
        beside = swap(send, "narrow", 1)
        far = add(far, beside[1])
        across = swap(far, "narrow", 2)
        stage.append((near, beside, across, pos, ids, meta))
    terms = []
    for c in range(groups):
        near, beside, across, pos, ids, meta = stage[c]
        keep, far, send = down(place, meta, ids, pos, near, beside, across, down_weight, GROUP, tok, width)
        beside = swap(send, "narrow", 1)
        parts = PARTS if c == groups - 1 else 1
        rows = GROUP * tok // parts
        for p in range(parts):
            own = slice(p * rows, (p + 1) * rows)
            across = swap(add(far[own], beside[1, own]), "narrow", 2)
            whole = add(keep[own], beside[0, own], across)
            for i in range(GROUP // parts):
                j = order[c][p * GROUP // parts + i]
                piece = whole[i * tok:(i + 1) * tok]
                terms.append(swap(piece, "wide", j) if j else piece)
    return add(*terms)


def solution(mesh):
    placed = (
        P("wide", "narrow"),
        P("narrow", None),
        P("wide", None, "narrow", None),
        P("wide", "narrow", None),
        P("wide", None),
    )

    return jax.shard_map(local, mesh=mesh, in_specs=placed, out_specs=P("wide", "narrow"), check_vma=False)
```
